768 devices in a mesh: seq: 96 (over x, z, core), head: 8 (over y).
Axes of the slice: x: 4, y: 8, z: 12, core: 2. Of those that a mesh axis runs over, the one named last changes fastest.
Arguments:
- queries: bfloat16 [24576, 2048], P('seq', 'head'), may hold values from -6 to 6
- keys: bfloat16 [24576, 2048], P('seq', 'head'), may hold values from -6 to 6
- values: bfloat16 [24576, 2048], P('seq', 'head'), may hold values from -6 to 6
- out_grad: bfloat16 [24576, 2048], P(('seq', 'head')), may hold values from -6 to 6
Outputs:
- attended: bfloat16 [24576, 2048], P('seq', 'head')
- query_grad: bfloat16 [24576, 2048], P('seq', 'head')
- key_grad: bfloat16 [24576, 2048], P('seq', 'head')
- value_grad: bfloat16 [24576, 2048], P('seq', 'head')
The draws below stay inside these ranges and needn't reach their ends.
All inputs are finite; a program needn't handle non-finite values.
Results may differ from the reference program's by a relative error of at most 0.0049.
Values may be sent and summed in bfloat16 or wider, within the bound.
A program may use at most 32 MiB of HBM per device.

```python
import math
import jax
import jax.numpy as jnp
from jax import lax

H = 32
DH = 64
BLOCK = 256
TOKENS = 24576


def steps_of(own_key, extent, pieces, least, largest):
    gain = 1.0
    for axis_at, shards_of in pieces:
        draws = jax.random.uniform(jax.random.fold_in(jax.random.fold_in(own_key, 6), axis_at), (shards_of,), jnp.float32, least / len(pieces), largest / len(pieces))
        gain = gain * jnp.repeat(jnp.exp(draws), extent[axis_at] // shards_of).reshape((-1,) + (1,) * (len(extent) - 1 - axis_at))
    return gain


def normal_values(rng, shape, width, most, cuts=(), kind=jnp.bfloat16):
    level = steps_of(rng, shape, cuts, -0.22, 0.18) if cuts else 1.0
    drawn = jax.random.normal(rng, shape, jnp.float32) * width * level
    return jnp.minimum(jnp.maximum(drawn, -most), most).astype(kind)


def setup_inputs(seed: int = 0) -> dict:
    arg_keys = jax.random.split(jax.random.key(seed), 5)
    return {
        "queries": normal_values(arg_keys[0], (TOKENS, H * DH), 1.0, 6.0, ((0, 96), (1, 8))),
        "keys": normal_values(arg_keys[1], (TOKENS, H * DH), 1.0, 6.0, ((0, 96), (1, 8))),
        "values": normal_values(arg_keys[2], (TOKENS, H * DH), 1.0, 6.0, ((0, 96), (1, 8))),
        "out_grad": normal_values(arg_keys[3], (TOKENS, H * DH), 1.0, 6.0, ((0, 768),)),
    }


def round_back(array):
    return lax.optimization_barrier(array.astype(jnp.bfloat16)).astype(jnp.float32)

def head_pass(parts):
    q_head, k_head, v_head, g_head = parts
    q_full = q_head.astype(jnp.float32)
    k_full = k_head.astype(jnp.float32)
    v_full = v_head.astype(jnp.float32)
    g_full = g_head.astype(jnp.float32)
    factor = 1.0 / math.sqrt(DH * TOKENS)
    causal = jnp.arange(BLOCK)[:, None] >= jnp.arange(BLOCK)[None, :]
    block_state = jnp.einsum('nta,ntb->nab', k_full, v_full)
    prefix_state = round_back(jnp.cumsum(block_state, 0) - block_state)
    grad_state = jnp.einsum('nta,ntb->nab', q_full, g_full)
    suffix_state = round_back(jnp.cumsum(grad_state[::-1], 0)[::-1] - grad_state)
    scores = jnp.einsum('nia,nja->nij', q_full, k_full) * factor
    probs = round_back(jnp.where(causal[None], scores, 0.0))
    attended = jnp.einsum('nij,njb->nib', probs, v_full) + factor * jnp.einsum('nia,nab->nib', q_full, prefix_state)
    dscores = jnp.einsum('nib,njb->nij', g_full, v_full) * factor
    dprobs = round_back(jnp.where(causal[None], dscores, 0.0))
    query_grad = jnp.einsum('nij,nja->nia', dprobs, k_full) + factor * jnp.einsum('nib,nab->nia', g_full, prefix_state)
    key_grad = jnp.einsum('nij,nia->nja', dprobs, q_full) + factor * jnp.einsum('njb,nab->nja', v_full, suffix_state)
    value_grad = jnp.einsum('nij,nib->njb', probs, g_full) + factor * jnp.einsum('nja,nab->njb', k_full, suffix_state)
    return (attended.astype(jnp.bfloat16), query_grad.astype(jnp.bfloat16), key_grad.astype(jnp.bfloat16), value_grad.astype(jnp.bfloat16))

def split_heads(array):
    blocks = TOKENS // BLOCK
    return array.reshape(blocks, BLOCK, H, DH).transpose(2, 0, 1, 3)

def join_heads(array):
    return array.transpose(1, 2, 0, 3).reshape(TOKENS, H * DH)

def reference(queries, keys, values, out_grad):
    results = lax.map(head_pass, (split_heads(queries), split_heads(keys), split_heads(values), split_heads(out_grad)))
    return (join_heads(results[0]), join_heads(results[1]), join_heads(results[2]), join_heads(results[3]))
```

```python
import functools
import math

import jax
import jax.numpy as jnp
from jax import lax
from jax.experimental import pallas as pl
from jax.experimental.pallas import tpu as pltpu
from jax.sharding import PartitionSpec as P

DH = 64
BLOCK = 256
PAIR = 2 * DH
MESH = pl.DeviceIdType.MESH

NX = 4
QUADS = 3
QUAD = 4

F32 = jnp.float32
BF16 = jnp.bfloat16


def dot(a, b):
    return lax.dot_general(a, b, (((1,), (0,)), ((), ())), preferred_element_type=F32)


def dot_t(a, b):
    return lax.dot_general(a, b, (((1,), (1,)), ((), ())), preferred_element_type=F32)


def t_dot(a, b):
    return lax.dot_general(a, b, (((0,), (0,)), ((), ())), preferred_element_type=F32)


def lane_half(shape):
    return lax.broadcasted_iota(jnp.int32, shape, 1) < DH


def compact(state):
    return jnp.where(lane_half((DH, PAIR)), state[:DH], state[DH:])


def spread(state):
    first = lane_half((DH, PAIR))
    zero = jnp.zeros_like(state)
    return jnp.concatenate([jnp.where(first, state, zero), jnp.where(first, zero, state)], 0)


def halves(a):
    first = lane_half(a.shape)
    zero = jnp.zeros_like(a)
    return jnp.where(first, a, zero), jnp.where(first, zero, a)


def carry_kernel(
    factor, ny,
    q_hbm, k_hbm, v_hbm, g_hbm,
    att, qg, kg_part, vg_part, k, v, suffix,
    q, g_rows, g, probs_t, att_part, qg_hold, local,
    state, core_in, chip_out, quad_in, quad_out, line_in, line_out, x_in, final_out, carried,
    load_sem, a2a_send, a2a_recv, send_sem, recv_sem,
):
    nz = QUADS * QUAD
    seq, head = lax.axis_index("seq"), lax.axis_index("head")
    core, chip = seq % 2, seq // 2
    x, z = chip // nz, chip % nz
    run, place = z // QUAD, z % QUAD
    rows = BLOCK // ny

    def at(x, run, place, core):
        return ((x * QUADS + run) * QUAD + place) * 2 + core

    mate = at(x, run, place, 1 - core)
    quad_mates = [at(x, run, (place + i) % QUAD, core) for i in range(1, QUAD)]
    line_mates = [at(x, (run + i) % QUADS, place, core) for i in range(1, QUADS)]
    x_mates = [at((x + i) % NX, run, place, core) for i in range(1, NX)]

    barrier = pltpu.get_barrier_semaphore()
    greeted = [mate] + quad_mates + line_mates + x_mates
    for other in range(1, ny):
        pl.semaphore_signal(
            barrier, inc=1, device_id=(seq, (head + other) % ny), device_id_type=MESH
        )
    for other in greeted:
        pl.semaphore_signal(barrier, inc=1, device_id=(other, head), device_id_type=MESH)

    loads = [
        pltpu.make_async_copy(src, dst, load_sem.at[i])
        for i, (src, dst) in enumerate(
            [(k_hbm, k), (v_hbm, v), (g_hbm, g_rows), (q_hbm, q)]
        )
    ]
    for load in loads:
        load.start()
    loads[0].wait()
    loads[1].wait()

    lanes = [pl.ds(p * PAIR, PAIR) for p in range(2)]
    for p in range(2):
        state[0, p] = compact(t_dot(k[:, lanes[p]], v[:, lanes[p]]))

    loads[2].wait()
    pl.semaphore_wait(barrier, ny - 1 + len(greeted))

    width = 2 * PAIR
    mine = pl.ds(pl.multiple_of(head * rows, rows), rows)
    exchange = []
    for i in sorted(range(1, ny), key=lambda i: -min(i, ny - i)):
        there = (head + i) % ny
        exchange.append(
            pltpu.make_async_remote_copy(
                src_ref=g_rows.at[:, pl.ds(pl.multiple_of(there * width, width), width)],
                dst_ref=g.at[mine, :],
                send_sem=a2a_send.at[i - 1],
                recv_sem=a2a_recv.at[i - 1],
                device_id=(seq, there),
                device_id_type=MESH,
            )
        )
        exchange[-1].start()
    own = pltpu.make_async_copy(
        g_rows.at[:, pl.ds(pl.multiple_of(head * width, width), width)],
        g.at[mine, :],
        load_sem.at[4],
    )
    own.start()

    sent = []

    def send(src, dst, slot, to):
        copy = pltpu.make_async_remote_copy(
            src_ref=src,
            dst_ref=dst,
            send_sem=send_sem.at[slot],
            recv_sem=recv_sem.at[slot],
            device_id=(to, head),
            device_id_type=MESH,
        )
        copy.start()
        sent.append(copy)
        return copy

    per_way = 2 + (QUAD - 1) + (QUADS - 1) + (NX - 1)

    def before(way, there, here):
        return there < here if way == 0 else there > here

    def masked(flag, value):
        return jnp.where(flag, value, jnp.zeros_like(value))

    def to_core(way):
        return [send(state.at[way, 1 - core], core_in.at[way], way * per_way, mate)]

    def to_quad(way, copies):
        copies[0].wait_recv()
        total = state[way, core] + core_in[way]
        local[way, 0] = total
        chip_out[way] = total.astype(BF16)
        base = way * per_way + 1
        return [
            send(chip_out.at[way], quad_in.at[way, i], base + i, to)
            for i, to in enumerate(quad_mates)
        ]

    def to_line(way, copies):
        for copy in copies:
            copy.wait_recv()
        total = local[way, 0]
        partial = jnp.zeros_like(total)
        for i in range(QUAD - 1):
            came = quad_in[way, i].astype(F32)
            total = total + came
            partial = partial + masked(before(way, (place - 1 - i) % QUAD, place), came)
        local[way, 0] = total
        local[way, 1] = partial
        quad_out[way] = total.astype(BF16)
        base = way * per_way + 1 + (QUAD - 1)
        return [
            send(quad_out.at[way], line_in.at[way, i], base + i, to)
            for i, to in enumerate(line_mates)
        ]

    def to_x(way, copies):
        for copy in copies:
            copy.wait_recv()
        total, partial = local[way, 0], local[way, 1]
        for i in range(QUADS - 1):
            came = line_in[way, i].astype(F32)
            total = total + came
            partial = partial + masked(before(way, (run - 1 - i) % QUADS, run), came)
        local[way, 1] = partial
        line_out[way] = total.astype(BF16)
        base = way * per_way + 1 + (QUAD - 1) + (QUADS - 1)
        return [
            send(line_out.at[way], x_in.at[way, i], base + i, to) for i, to in enumerate(x_mates)
        ]

    def to_mate(way, copies):
        for copy in copies:
            copy.wait_recv()
        partial = local[way, 1]
        for i in range(NX - 1):
            came = x_in[way, i].astype(F32)
            partial = partial + masked(before(way, (x - 1 - i) % NX, x), came)
        carries = core == 1 - way
        here = partial + masked(carries, core_in[way])
        there = partial + masked(jnp.logical_not(carries), state[way, core])
        final_out[way] = there.astype(BF16)
        copy = send(
            final_out.at[way], carried.at[way, core], way * per_way + per_way - 1, mate
        )
        carried[way, core] = here.astype(BF16)
        return [copy]

    row = lax.broadcasted_iota(jnp.int32, (BLOCK, BLOCK), 0)
    col = lax.broadcasted_iota(jnp.int32, (BLOCK, BLOCK), 1)
    lower, upper = row >= col, row <= col

    def weights(a, b, keep):
        return jnp.where(keep, dot_t(a, b) * factor, 0.0).astype(BF16)

    def forward_part():
        for p in range(2):
            qs, ks, vs = q[:, lanes[p]], k[:, lanes[p]], v[:, lanes[p]]
            kh, vh = halves(ks), halves(vs)
            total = jnp.zeros((BLOCK, PAIR), F32)
            for h in range(2):
                total += dot(weights(qs, kh[h], lower), vh[h])
                probs_t[2 * p + h] = weights(kh[h], qs, upper)
            att_part[:, lanes[p]] = total

    def backward_part():
        for p in range(2):
            qs, ks, vs, gs = (a[:, lanes[p]] for a in (q, k, v, g))
            qh, kh, vh, gh = halves(qs), halves(ks), halves(vs), halves(gs)
            q_sum = jnp.zeros((BLOCK, PAIR), F32)
            k_sum = jnp.zeros((BLOCK, PAIR), F32)
            v_sum = jnp.zeros((BLOCK, PAIR), F32)
            for h in range(2):
                q_sum += dot(weights(gs, vh[h], lower), kh[h])
                k_sum += dot(weights(vh[h], gs, upper), qh[h])
                v_sum += dot(probs_t[2 * p + h], gh[h])
            qg_hold[:, lanes[p]] = q_sum
            kg_part[:, lanes[p]] = k_sum
            vg_part[:, lanes[p]] = v_sum

    forward = to_core(0)
    forward = to_quad(0, forward)
    loads[3].wait()
    forward_part()
    forward = to_line(0, forward)

    own.wait()
    for copy in exchange:
        copy.wait_recv()
    for p in range(2):
        state[1, p] = compact(t_dot(q[:, lanes[p]], g[:, lanes[p]]))
    backward = to_core(1)
    backward = to_quad(1, backward)
    forward = to_x(0, forward)
    backward_part()
    backward = to_line(1, backward)
    forward = to_mate(0, forward)
    forward[0].wait_recv()
    for p in range(2):
        prefix = spread(carried[0, p])
        att[:, lanes[p]] = (att_part[:, lanes[p]] + factor * dot(q[:, lanes[p]], prefix)).astype(BF16)
        qg[:, lanes[p]] = (qg_hold[:, lanes[p]] + factor * dot_t(g[:, lanes[p]], prefix)).astype(BF16)
    backward = to_x(1, backward)
    backward = to_mate(1, backward)
    for copy in exchange + sent:
        copy.wait_send()
    backward[0].wait_recv()
    suffix[...] = carried[1]


def finish_kernel(factor, att_in, qg_in, kg_part, vg_part, k, v, suffix, att, qg, kg, vg, kg_out, vg_out, sem):
    done = [
        pltpu.make_async_copy(att_in, att, sem.at[0]),
        pltpu.make_async_copy(qg_in, qg, sem.at[1]),
    ]
    for copy in done:
        copy.start()
    for p in range(2):
        lanes = pl.ds(p * PAIR, PAIR)
        later = spread(suffix[p])
        kg_out[:, lanes] = (kg_part[:, lanes] + factor * dot_t(v[:, lanes], later)).astype(BF16)
        vg_out[:, lanes] = (vg_part[:, lanes] + factor * dot(k[:, lanes], later)).astype(BF16)
    for i, (src, dst) in enumerate([(kg_out, kg), (vg_out, vg)]):
        done.append(pltpu.make_async_copy(src, dst, sem.at[2 + i]))
        done[-1].start()
    for copy in done:
        copy.wait()


def on_device(queries, keys, values, out_grad):
    ny = lax.axis_size("head")
    tokens = queries.shape[0] * lax.axis_size("seq")
    factor = 1.0 / math.sqrt(DH * tokens)
    wide = queries.shape
    vmem = pl.BlockSpec(memory_space=pltpu.VMEM)
    hbm = pl.BlockSpec(memory_space=pltpu.HBM)
    messages = 2 * (2 + (QUAD - 1) + (QUADS - 1) + (NX - 1))
    pair = (DH, PAIR)
    held = pl.pallas_call(
        functools.partial(carry_kernel, factor, ny),
        out_shape=[
            jax.ShapeDtypeStruct(wide, BF16),
            jax.ShapeDtypeStruct(wide, BF16),
            jax.ShapeDtypeStruct(wide, F32),
            jax.ShapeDtypeStruct(wide, F32),
            jax.ShapeDtypeStruct(wide, BF16),
            jax.ShapeDtypeStruct(wide, BF16),
            jax.ShapeDtypeStruct((2,) + pair, BF16),
        ],
        in_specs=[hbm] * 4,
        out_specs=[vmem] * 7,
        scratch_shapes=[
            pltpu.VMEM(wide, BF16),
            pltpu.VMEM(out_grad.shape, BF16),
            pltpu.VMEM(wide, BF16),
            pltpu.VMEM((4, BLOCK, BLOCK), BF16),
            pltpu.VMEM(wide, F32),
            pltpu.VMEM(wide, F32),
            pltpu.VMEM((2, 2) + pair, F32),
            pltpu.VMEM((2, 2) + pair, F32),
            pltpu.VMEM((2,) + pair, F32),
            pltpu.VMEM((2,) + pair, BF16),
            pltpu.VMEM((2, QUAD - 1) + pair, BF16),
            pltpu.VMEM((2,) + pair, BF16),
            pltpu.VMEM((2, QUADS - 1) + pair, BF16),
            pltpu.VMEM((2,) + pair, BF16),
            pltpu.VMEM((2, NX - 1) + pair, BF16),
            pltpu.VMEM((2,) + pair, BF16),
            pltpu.VMEM((2, 2) + pair, BF16),
            pltpu.SemaphoreType.DMA((5,)),
            pltpu.SemaphoreType.DMA((ny - 1,)),
            pltpu.SemaphoreType.DMA((ny - 1,)),
            pltpu.SemaphoreType.DMA((messages,)),
            pltpu.SemaphoreType.DMA((messages,)),
        ],
        compiler_params=pltpu.CompilerParams(
            collective_id=0, has_side_effects=True, vmem_limit_bytes=16 << 20
        ),
        name="carry",
    )(*[pltpu.with_memory_space_constraint(a, pltpu.HBM) for a in (queries, keys, values, out_grad)])
    return pl.pallas_call(
        functools.partial(finish_kernel, factor),
        out_shape=[jax.ShapeDtypeStruct(wide, BF16)] * 4,
        in_specs=[vmem] * 7,
        out_specs=[hbm] * 4,
        scratch_shapes=[
            pltpu.VMEM(wide, BF16),
            pltpu.VMEM(wide, BF16),
            pltpu.SemaphoreType.DMA((4,)),
        ],
        compiler_params=pltpu.CompilerParams(vmem_limit_bytes=16 << 20),
        name="finish",
    )(*held)


def solution(mesh):
    split = P("seq", "head")
    return jax.shard_map(
        on_device,
        mesh=mesh,
        in_specs=(split, split, split, P(("seq", "head"), None)),
        out_specs=(split, split, split, split),
        check_vma=False,
    )
```

```python
import functools
import math

import jax
import jax.numpy as jnp
from jax import lax
from jax.experimental import pallas as pl
from jax.experimental.pallas import tpu as pltpu
from jax.sharding import PartitionSpec as P

DH = 64
BLOCK = 256
PAIR = 2 * DH
MESH = pl.DeviceIdType.MESH

NX = 4
QUADS = 3
QUAD = 4
NZ = QUADS * QUAD
REACH = 4
ROUNDS = 1

F32 = jnp.float32
BF16 = jnp.bfloat16


def dot(a, b):
    return lax.dot_general(a, b, (((1,), (0,)), ((), ())), preferred_element_type=F32)


def dot_t(a, b):
    return lax.dot_general(a, b, (((1,), (1,)), ((), ())), preferred_element_type=F32)


def t_dot(a, b):
    return lax.dot_general(a, b, (((0,), (0,)), ((), ())), preferred_element_type=F32)


def lane_half(shape):
    return lax.broadcasted_iota(jnp.int32, shape, 1) < DH


def compact(state):
    return jnp.where(lane_half((DH, PAIR)), state[:DH], state[DH:])


def spread(state):
    first = lane_half((DH, PAIR))
    zero = jnp.zeros_like(state)
    return jnp.concatenate([jnp.where(first, state, zero), jnp.where(first, zero, state)], 0)


def halves(a):
    first = lane_half(a.shape)
    zero = jnp.zeros_like(a)
    return jnp.where(first, a, zero), jnp.where(first, zero, a)


def carry_kernel(
    factor, ny,
    q_hbm, k_hbm, v_hbm, g_hbm,
    att, qg, kg_part, vg_part, k, v, suffix,
    q, q_mate, g_pair, g, probs_t, att_part, qg_part,
    state, core_in, chip, chip_out, quad_in, sums, quad_out, line_in, z_in, x_out, x_in, rest_out, rest_in, total,
    load_sem, a2a_send, a2a_recv, core_send, core_recv, quad_send, quad_recv, line_send, line_recv, z_send, z_recv, x_send, x_recv,
    rest_send, rest_recv, heard,
):
    seq, head = lax.axis_index("seq"), lax.axis_index("head")
    core, chip_id = seq % 2, seq // 2
    x, z = chip_id // NZ, chip_id % NZ
    run, place = z // QUAD, z % QUAD
    rows = BLOCK // ny

    def at(x, z, core):
        return (x * NZ + z) * 2 + core

    mate = at(x, z, 1 - core)

    barrier = pltpu.get_barrier_semaphore()
    greeted = [(to, (head + i) % ny) for i in range(1, ny) for to in (seq, mate)] + [(mate, head)]
    near = sorted({i % NZ for i in range(-REACH, REACH + 1)} - {0})
    greeted += [(at(x, (z + i) % NZ, core), head) for i in near]
    greeted += [(at((x + i) % NX, z, c), head) for i in range(1, NX) for c in range(2)]
    for other in greeted:
        pl.semaphore_signal(barrier, inc=1, device_id=other, device_id_type=MESH)

    loads = [
        pltpu.make_async_copy(src, dst, load_sem.at[i])
        for i, (src, dst) in enumerate(
            [(k_hbm, k), (v_hbm, v), (q_hbm, q)]
        )
    ]
    for load in loads:
        load.start()
    pl.semaphore_wait(barrier, len(greeted))

    def tell(turn):
        for i, step in enumerate((REACH, NZ - REACH)):
            to = (at(x, (z + step) % NZ, core), head)
            pl.semaphore_signal(heard.at[turn, i], inc=1, device_id=to, device_id_type=MESH)

    def hear(turn):
        for i in range(2):
            pl.semaphore_wait(heard.at[turn, i], 1)

    mine = pl.ds(pl.multiple_of(head * rows, rows), rows)

    def columns(group, pair):
        return pl.ds(pl.multiple_of((2 * group + pair) * PAIR, PAIR), PAIR)

    exchange = []
    for i in sorted(range(ny), key=lambda i: -min(i, ny - i)):
        there = (head + i) % ny
        for j in range(2):
            if i == 0 and j == 0:
                continue
            exchange.append(
                pltpu.make_async_remote_copy(
                    src_ref=g_hbm.at[:, columns(there, (core + j) % 2)],
                    dst_ref=g_pair.at[core, mine, :],
                    send_sem=a2a_send.at[2 * i + j],
                    recv_sem=a2a_recv.at[2 * i + j],
                    device_id=(at(x, z, (core + j) % 2), there),
                    device_id_type=MESH,
                )
            )
            exchange[-1].start()
    own = pltpu.make_async_copy(
        g_hbm.at[:, columns(head, core)], g_pair.at[core, mine, :], load_sem.at[4]
    )
    own.start()
    tell(0)

    loads[0].wait()
    loads[1].wait()

    lanes = [pl.ds(p * PAIR, PAIR) for p in range(2)]
    for p in range(2):
        state[0, p] = compact(t_dot(k[:, lanes[p]], v[:, lanes[p]]))


    sent = []

    def send(src, dst, send_sem, recv_sem, to, when=None):
        copy = pltpu.make_async_remote_copy(
            src_ref=src,
            dst_ref=dst,
            send_sem=send_sem,
            recv_sem=recv_sem,
            device_id=(to, head),
            device_id_type=MESH,
        )
        if when is None:
            copy.start()
        else:
            pl.when(when)(copy.start)
        sent.append((when, copy))
        return copy

    def arrived(ref, sem):
        pltpu.make_async_copy(ref, ref, sem).wait()

    def masked(flag, value):
        return jnp.where(flag, value, jnp.zeros_like(value))

    def before(way, there, here):
        return there < here if way == 0 else there > here

    def half(core):
        return pl.ds(pl.multiple_of(core * PAIR, PAIR), PAIR)

    def chip_sum(way):
        both = state[way, core] + core_in[way]
        chip[way] = both
        chip_out[way] = both.astype(BF16)

    def to_quad():
        arrived(core_in.at[0], core_recv.at[0])
        chip_sum(0)
        for i in range(QUAD - 1):
            send(
                chip_out.at[0], quad_in.at[i], quad_send.at[i], quad_recv.at[i],
                at(x, run * QUAD + (place + 1 + i) % QUAD, core),
            )

    def to_line():
        for i in range(QUAD - 1):
            arrived(quad_in.at[i], quad_recv.at[i])
        whole = chip[0]
        partial = jnp.zeros((DH, PAIR), F32)
        for i in range(QUAD - 1):
            came = quad_in[i].astype(F32)
            whole += came
            partial += masked((place - 1 - i) % QUAD < place, came)
        sums[0] = whole
        sums[1] = partial
        quad_out[...] = whole.astype(BF16)
        for i in range(QUADS - 1):
            send(
                quad_out, line_in.at[i], line_send.at[i], line_recv.at[i],
                at(x, (run + 1 + i) % QUADS * QUAD + place, core),
            )

    def earlier():
        for i in range(QUADS - 1):
            arrived(line_in.at[i], line_recv.at[i])
        whole, partial = sums[0], sums[1]
        for i in range(QUADS - 1):
            came = line_in[i].astype(F32)
            whole += came
            partial += masked((run - 1 - i) % QUADS < run, came)
        return whole, partial

    def to_all():
        chip_sum(1)
        for there in range(NZ):
            send(
                chip_out.at[1], z_in.at[z], z_send.at[there], z_recv.at[z], at(x, there, core),
                jnp.logical_or(there < z, jnp.logical_and(there > z, x > 0)),
            )

    def later():
        whole_acc = sums.at[2]
        part_acc = sums.at[3]
        whole_acc[...] = chip[1]
        part_acc[...] = jnp.zeros((DH, PAIR), F32)
        for there in range(NZ):

            @pl.when(there > z)
            def _():
                arrived(z_in.at[there], z_recv.at[there])
                came = z_in[there].astype(F32)
                whole_acc[...] += came
                part_acc[...] += came

            @pl.when(jnp.logical_and(there < z, x > 0))
            def _():
                arrived(z_in.at[there], z_recv.at[there])
                whole_acc[...] += z_in[there].astype(F32)

        return whole_acc[...], part_acc[...]

    def to_x(way):
        whole, partial = (earlier, later)[way]()
        x_out[way] = whole.astype(BF16)
        for there in range(NX):
            for c in range(2):
                send(
                    x_out.at[way], x_in.at[way, core, x],
                    x_send.at[way, there, c], x_recv.at[way, core, x],
                    at(there, z, c), before(way, x, there),
                )
        carries = core == 1 - way
        total[way, core] = partial + masked(carries, core_in[way])
        rest_out[way] = partial + masked(jnp.logical_not(carries), state[way, core])
        send(rest_out.at[way], rest_in.at[way], rest_send.at[way], rest_recv.at[way], mate)

    def finish(way):
        arrived(rest_in.at[way], rest_recv.at[way])
        total[way, 1 - core] = rest_in[way]
        for there in range(NX):

            @pl.when(before(way, there, x))
            def _():
                for p in range(2):
                    arrived(x_in.at[way, p, there], x_recv.at[way, p, there])
                for p in range(2):
                    total[way, p] += x_in[way, p, there].astype(F32)

    row = lax.broadcasted_iota(jnp.int32, (BLOCK, BLOCK), 0)
    col = lax.broadcasted_iota(jnp.int32, (BLOCK, BLOCK), 1)
    lower, upper = row >= col, row <= col

    def weights(a, b, keep):
        return jnp.where(keep, dot_t(a, b) * factor, 0.0).astype(BF16)

    def forward_part():
        for p in range(2):
            qs, ks, vs = q[:, lanes[p]], k[:, lanes[p]], v[:, lanes[p]]
            kh, vh = halves(ks), halves(vs)
            acc = jnp.zeros((BLOCK, PAIR), F32)
            for h in range(2):
                acc += dot(weights(qs, kh[h], lower), vh[h])
                probs_t[2 * p + h] = weights(kh[h], qs, upper)
            att_part[:, lanes[p]] = acc

    def backward_part():
        for p in range(2):
            qs, ks, vs = (a[:, lanes[p]] for a in (q, k, v))
            gs = g[p]
            qh, kh, vh, gh = halves(qs), halves(ks), halves(vs), halves(gs)
            q_sum = jnp.zeros((BLOCK, PAIR), F32)
            k_sum = jnp.zeros((BLOCK, PAIR), F32)
            v_sum = jnp.zeros((BLOCK, PAIR), F32)
            for h in range(2):
                q_sum += dot(weights(gs, vh[h], lower), kh[h])
                k_sum += dot(weights(vh[h], gs, upper), qh[h])
                v_sum += dot(probs_t[2 * p + h], gh[h])
            qg_part[:, lanes[p]] = q_sum
            kg_part[:, lanes[p]] = k_sum
            vg_part[:, lanes[p]] = v_sum

    send(state.at[0, 1 - core], core_in.at[0], core_send.at[0], core_recv.at[0], mate)
    loads[2].wait()
    send(q.at[:, half(1 - core)], q_mate, core_send.at[1], core_recv.at[1], mate)
    forward_part()
    to_quad()
    for turn in range(ROUNDS):
        hear(turn)
        if turn + 1 < ROUNDS:
            tell(turn + 1)
    to_line()

    arrived(q_mate, core_recv.at[1])
    own.wait()
    for copy in exchange:
        copy.wait_recv()
    state[1, core] = compact(t_dot(q[:, half(core)], g_pair[core]))
    core_in[1] = compact(t_dot(q_mate[...], g_pair[1 - core]))
    to_all()
    send(g_pair.at[1 - core], g.at[core], core_send.at[2], core_recv.at[2], mate)
    g[core] = g_pair[core]
    arrived(g.at[1 - core], core_recv.at[2])
    backward_part()

    to_x(0)
    to_x(1)
    finish(0)
    for p in range(2):
        prefix = spread(total[0, p].astype(BF16))
        att[:, lanes[p]] = (att_part[:, lanes[p]] + factor * dot(q[:, lanes[p]], prefix)).astype(BF16)
        qg[:, lanes[p]] = (qg_part[:, lanes[p]] + factor * dot_t(g[p], prefix)).astype(BF16)
    for copy in exchange:
        copy.wait_send()
    for when, copy in sent:
        if when is None:
            copy.wait_send()
        else:
            pl.when(when)(copy.wait_send)
    finish(1)
    suffix[...] = total[1].astype(BF16)


def finish_kernel(factor, att_in, qg_in, kg_part, vg_part, k, v, suffix, att, qg, kg, vg, kg_out, vg_out, sem):
    done = [
        pltpu.make_async_copy(att_in, att, sem.at[0]),
        pltpu.make_async_copy(qg_in, qg, sem.at[1]),
    ]
    for copy in done:
        copy.start()
    for p in range(2):
        lanes = pl.ds(p * PAIR, PAIR)
        later = spread(suffix[p])
        kg_out[:, lanes] = (kg_part[:, lanes] + factor * dot_t(v[:, lanes], later)).astype(BF16)
        vg_out[:, lanes] = (vg_part[:, lanes] + factor * dot(k[:, lanes], later)).astype(BF16)
    for i, (src, dst) in enumerate([(kg_out, kg), (vg_out, vg)]):
        done.append(pltpu.make_async_copy(src, dst, sem.at[2 + i]))
        done[-1].start()
    for copy in done:
        copy.wait()


def on_device(queries, keys, values, out_grad):
    ny = lax.axis_size("head")
    tokens = queries.shape[0] * lax.axis_size("seq")
    factor = 1.0 / math.sqrt(DH * tokens)
    wide = queries.shape
    vmem = pl.BlockSpec(memory_space=pltpu.VMEM)
    hbm = pl.BlockSpec(memory_space=pltpu.HBM)
    pair = (DH, PAIR)
    held = pl.pallas_call(
        functools.partial(carry_kernel, factor, ny),
        out_shape=[
            jax.ShapeDtypeStruct(wide, BF16),
            jax.ShapeDtypeStruct(wide, BF16),
            jax.ShapeDtypeStruct(wide, F32),
            jax.ShapeDtypeStruct(wide, F32),
            jax.ShapeDtypeStruct(wide, BF16),
            jax.ShapeDtypeStruct(wide, BF16),
            jax.ShapeDtypeStruct((2,) + pair, BF16),
        ],
        in_specs=[hbm] * 4,
        out_specs=[vmem] * 7,
        scratch_shapes=[
            pltpu.VMEM(wide, BF16),
            pltpu.VMEM((BLOCK, PAIR), BF16),
            pltpu.VMEM((2, BLOCK, PAIR), BF16),
            pltpu.VMEM((2, BLOCK, PAIR), BF16),
            pltpu.VMEM((4, BLOCK, BLOCK), BF16),
            pltpu.VMEM(wide, F32),
            pltpu.VMEM(wide, F32),
            pltpu.VMEM((2, 2) + pair, F32),
            pltpu.VMEM((2,) + pair, F32),
            pltpu.VMEM((2,) + pair, F32),
            pltpu.VMEM((2,) + pair, BF16),
            pltpu.VMEM((QUAD - 1,) + pair, BF16),
            pltpu.VMEM((4,) + pair, F32),
            pltpu.VMEM(pair, BF16),
            pltpu.VMEM((QUADS - 1,) + pair, BF16),
            pltpu.VMEM((NZ,) + pair, BF16),
            pltpu.VMEM((2,) + pair, BF16),
            pltpu.VMEM((2, 2, NX) + pair, BF16),
            pltpu.VMEM((2,) + pair, F32),
            pltpu.VMEM((2,) + pair, F32),
            pltpu.VMEM((2, 2) + pair, F32),
            pltpu.SemaphoreType.DMA((5,)),
            pltpu.SemaphoreType.DMA((2 * ny,)),
            pltpu.SemaphoreType.DMA((2 * ny,)),
            pltpu.SemaphoreType.DMA((3,)),
            pltpu.SemaphoreType.DMA((3,)),
            pltpu.SemaphoreType.DMA((QUAD - 1,)),
            pltpu.SemaphoreType.DMA((QUAD - 1,)),
            pltpu.SemaphoreType.DMA((QUADS - 1,)),
            pltpu.SemaphoreType.DMA((QUADS - 1,)),
            pltpu.SemaphoreType.DMA((NZ,)),
            pltpu.SemaphoreType.DMA((NZ,)),
            pltpu.SemaphoreType.DMA((2, NX, 2)),
            pltpu.SemaphoreType.DMA((2, 2, NX)),
            pltpu.SemaphoreType.DMA((2,)),
            pltpu.SemaphoreType.DMA((2,)),
            pltpu.SemaphoreType.REGULAR((ROUNDS, 2)),
        ],
        compiler_params=pltpu.CompilerParams(
            collective_id=0, has_side_effects=True, vmem_limit_bytes=16 << 20
        ),
        name="carry",
    )(*[pltpu.with_memory_space_constraint(a, pltpu.HBM) for a in (queries, keys, values, out_grad)])
    return pl.pallas_call(
        functools.partial(finish_kernel, factor),
        out_shape=[jax.ShapeDtypeStruct(wide, BF16)] * 4,
        in_specs=[vmem] * 7,
        out_specs=[hbm] * 4,
        scratch_shapes=[
            pltpu.VMEM(wide, BF16),
            pltpu.VMEM(wide, BF16),
            pltpu.SemaphoreType.DMA((4,)),
        ],
        compiler_params=pltpu.CompilerParams(vmem_limit_bytes=16 << 20),
        name="finish",
    )(*held)


def solution(mesh):
    split = P("seq", "head")
    return jax.shard_map(
        on_device,
        mesh=mesh,
        in_specs=(split, split, split, P(("seq", "head"), None)),
        out_specs=(split, split, split, split),
        check_vma=False,
    )
```

```python
import functools
import math

import jax
import jax.numpy as jnp
from jax import lax
from jax.experimental import pallas as pl
from jax.experimental.pallas import tpu as pltpu
from jax.sharding import PartitionSpec as P

DH = 64
BLOCK = 256
PAIR = 2 * DH
MESH = pl.DeviceIdType.MESH

NX = 4
QUADS = 3
QUAD = 4
NZ = QUADS * QUAD
REACH = 4
ROUNDS = 1

F32 = jnp.float32
BF16 = jnp.bfloat16


def dot(a, b):
    return lax.dot_general(a, b, (((1,), (0,)), ((), ())), preferred_element_type=F32)


def dot_t(a, b):
    return lax.dot_general(a, b, (((1,), (1,)), ((), ())), preferred_element_type=F32)


def t_dot(a, b):
    return lax.dot_general(a, b, (((0,), (0,)), ((), ())), preferred_element_type=F32)


def lane_half(shape):
    return lax.broadcasted_iota(jnp.int32, shape, 1) < DH


def compact(state):
    return jnp.where(lane_half((DH, PAIR)), state[:DH], state[DH:])


def spread(state):
    first = lane_half((DH, PAIR))
    zero = jnp.zeros_like(state)
    return jnp.concatenate([jnp.where(first, state, zero), jnp.where(first, zero, state)], 0)


def halves(a):
    first = lane_half(a.shape)
    zero = jnp.zeros_like(a)
    return jnp.where(first, a, zero), jnp.where(first, zero, a)


def carry_kernel(
    factor, ny,
    q_hbm, k_hbm, v_hbm, g_hbm,
    att, qg, kg_part, vg_part, k, v, suffix,
    q, q_mate, g_pair, g, probs_t, att_part, qg_part,
    state, core_in, chip, chip_out, quad_in, sums, quad_out, line_in, z_in, x_out, x_in, rest_out, rest_in, total,
    load_sem, a2a_send, a2a_recv, core_send, core_recv, quad_send, quad_recv, line_send, line_recv, z_send, z_recv, x_send, x_recv,
    rest_send, rest_recv, heard,
):
    seq, head = lax.axis_index("seq"), lax.axis_index("head")
    core, chip_id = seq % 2, seq // 2
    x, z = chip_id // NZ, chip_id % NZ
    run, place = z // QUAD, z % QUAD
    rows = BLOCK // ny

    def at(x, z, core):
        return (x * NZ + z) * 2 + core

    mate = at(x, z, 1 - core)

    barrier = pltpu.get_barrier_semaphore()
    greeted = [(to, (head + i) % ny) for i in range(1, ny) for to in (seq, mate)] + [(mate, head)]
    near = sorted({i % NZ for i in range(-REACH, REACH + 1)} - {0})
    greeted += [(at(x, (z + i) % NZ, core), head) for i in near]
    greeted += [(at((x + i) % NX, z, c), head) for i in range(1, NX) for c in range(2)]
    for other in greeted:
        pl.semaphore_signal(barrier, inc=1, device_id=other, device_id_type=MESH)

    loads = [
        pltpu.make_async_copy(src, dst, load_sem.at[i])
        for i, (src, dst) in enumerate(
            [(k_hbm, k), (v_hbm, v), (q_hbm, q)]
        )
    ]
    for load in loads:
        load.start()
    pl.semaphore_wait(barrier, len(greeted))

    def tell(turn):
        for i, step in enumerate((REACH, NZ - REACH)):
            to = (at(x, (z + step) % NZ, core), head)
            pl.semaphore_signal(heard.at[turn, i], inc=1, device_id=to, device_id_type=MESH)

    def hear(turn):
        for i in range(2):
            pl.semaphore_wait(heard.at[turn, i], 1)

    mine = pl.ds(pl.multiple_of(head * rows, rows), rows)

    def columns(group, pair):
        return pl.ds(pl.multiple_of((2 * group + pair) * PAIR, PAIR), PAIR)

    exchange = []
    for i in sorted(range(ny), key=lambda i: -min(i, ny - i)):
        there = (head + i) % ny
        for j in range(2):
            if i == 0 and j == 0:
                continue
            exchange.append(
                pltpu.make_async_remote_copy(
                    src_ref=g_hbm.at[:, columns(there, (core + j) % 2)],
                    dst_ref=g_pair.at[core, mine, :],
                    send_sem=a2a_send.at[2 * i + j],
                    recv_sem=a2a_recv.at[2 * i + j],
                    device_id=(at(x, z, (core + j) % 2), there),
                    device_id_type=MESH,
                )
            )
            exchange[-1].start()
    own = pltpu.make_async_copy(
        g_hbm.at[:, columns(head, core)], g_pair.at[core, mine, :], load_sem.at[4]
    )
    own.start()
    tell(0)

    loads[0].wait()
    loads[1].wait()

    lanes = [pl.ds(p * PAIR, PAIR) for p in range(2)]
    for p in range(2):
        state[0, p] = compact(t_dot(k[:, lanes[p]], v[:, lanes[p]]))


    sent = []

    def send(src, dst, send_sem, recv_sem, to):
        copy = pltpu.make_async_remote_copy(
            src_ref=src,
            dst_ref=dst,
            send_sem=send_sem,
            recv_sem=recv_sem,
            device_id=(to, head),
            device_id_type=MESH,
        )
        copy.start()
        sent.append((None, [copy]))

    def settle():
        for when, copies in sent:
            if when is None:
                copies[0].wait_send()
                continue

            @pl.when(when)
            def _():
                for copy in copies:
                    copy.wait_send()

        sent.clear()

    def arrived(ref, sem):
        pltpu.make_async_copy(ref, ref, sem).wait()

    def masked(flag, value):
        return jnp.where(flag, value, jnp.zeros_like(value))

    def before(way, there, here):
        return there < here if way == 0 else there > here

    def half(core):
        return pl.ds(pl.multiple_of(core * PAIR, PAIR), PAIR)

    def chip_sum(way):
        both = state[way, core] + core_in[way]
        chip[way] = both
        chip_out[way] = both.astype(BF16)

    def to_quad():
        arrived(core_in.at[0], core_recv.at[0])
        chip_sum(0)
        for i in range(QUAD - 1):
            send(
                chip_out.at[0], quad_in.at[i], quad_send.at[i], quad_recv.at[i],
                at(x, run * QUAD + (place + 1 + i) % QUAD, core),
            )

    def to_line():
        for i in range(QUAD - 1):
            arrived(quad_in.at[i], quad_recv.at[i])
        whole = chip[0]
        partial = jnp.zeros((DH, PAIR), F32)
        for i in range(QUAD - 1):
            came = quad_in[i].astype(F32)
            whole += came
            partial += masked((place - 1 - i) % QUAD < place, came)
        sums[0] = whole
        sums[1] = partial
        quad_out[...] = whole.astype(BF16)
        for i in range(QUADS - 1):
            send(
                quad_out, line_in.at[i], line_send.at[i], line_recv.at[i],
                at(x, (run + 1 + i) % QUADS * QUAD + place, core),
            )

    def earlier():
        for i in range(QUADS - 1):
            arrived(line_in.at[i], line_recv.at[i])
        whole, partial = sums[0], sums[1]
        for i in range(QUADS - 1):
            came = line_in[i].astype(F32)
            whole += came
            partial += masked((run - 1 - i) % QUADS < run, came)
        return whole, partial

    turn_from = jnp.maximum(z - 2, 0)
    others = [jnp.where(z == 0, 1, 0), jnp.where(z <= 1, 2, 1)]
    others += [2 + (turn_from + i) % (NZ - 2) for i in range(1, NZ - 2)]

    def to_all():
        chip_sum(1)
        for i, there in enumerate(others):
            send(chip_out.at[1], z_in.at[z], z_send.at[i], z_recv.at[z], at(x, there, core))

    def later():
        for there in others:
            arrived(z_in.at[there], z_recv.at[there])
        whole = chip[1]
        partial = jnp.zeros((DH, PAIR), F32)
        for there in others:
            came = z_in[there].astype(F32)
            whole += came
            partial += masked(there > z, came)
        return whole, partial

    def to_x(way):
        whole, partial = (earlier, later)[way]()
        x_out[way] = whole.astype(BF16)
        for there in range(1, NX) if way == 0 else range(NX - 1):
            copies = [
                pltpu.make_async_remote_copy(
                    src_ref=x_out.at[way],
                    dst_ref=x_in.at[way, core, x],
                    send_sem=x_send.at[way, there, c],
                    recv_sem=x_recv.at[way, core, x],
                    device_id=(at(there, z, c), head),
                    device_id_type=MESH,
                )
                for c in range(2)
            ]

            @pl.when(before(way, x, there))
            def _():
                for copy in copies:
                    copy.start()

            sent.append((before(way, x, there), copies))
        carries = core == 1 - way
        total[way, core] = partial + masked(carries, core_in[way])
        rest_out[way] = partial + masked(jnp.logical_not(carries), state[way, core])
        send(rest_out.at[way], rest_in.at[way], rest_send.at[way], rest_recv.at[way], mate)

    def finish(way):
        arrived(rest_in.at[way], rest_recv.at[way])
        total[way, 1 - core] = rest_in[way]
        for there in range(NX - 1) if way == 0 else range(1, NX):

            @pl.when(before(way, there, x))
            def _():
                for p in range(2):
                    arrived(x_in.at[way, p, there], x_recv.at[way, p, there])
                for p in range(2):
                    total[way, p] += x_in[way, p, there].astype(F32)

    row = lax.broadcasted_iota(jnp.int32, (BLOCK, BLOCK), 0)
    col = lax.broadcasted_iota(jnp.int32, (BLOCK, BLOCK), 1)
    lower, upper = row >= col, row <= col

    def weights(a, b, keep):
        return jnp.where(keep, dot_t(a, b) * factor, 0.0).astype(BF16)

    def forward_part():
        for p in range(2):
            qs, ks, vs = q[:, lanes[p]], k[:, lanes[p]], v[:, lanes[p]]
            kh, vh = halves(ks), halves(vs)
            acc = jnp.zeros((BLOCK, PAIR), F32)
            for h in range(2):
                acc += dot(weights(qs, kh[h], lower), vh[h])
                probs_t[2 * p + h] = weights(kh[h], qs, upper)
            att_part[:, lanes[p]] = acc

    def backward_part():
        for p in range(2):
            qs, ks, vs = (a[:, lanes[p]] for a in (q, k, v))
            gs = g[p]
            qh, kh, vh, gh = halves(qs), halves(ks), halves(vs), halves(gs)
            q_sum = jnp.zeros((BLOCK, PAIR), F32)
            k_sum = jnp.zeros((BLOCK, PAIR), F32)
            v_sum = jnp.zeros((BLOCK, PAIR), F32)
            for h in range(2):
                q_sum += dot(weights(gs, vh[h], lower), kh[h])
                k_sum += dot(weights(vh[h], gs, upper), qh[h])
                v_sum += dot(probs_t[2 * p + h], gh[h])
            qg_part[:, lanes[p]] = q_sum
            kg_part[:, lanes[p]] = k_sum
            vg_part[:, lanes[p]] = v_sum

    send(state.at[0, 1 - core], core_in.at[0], core_send.at[0], core_recv.at[0], mate)
    loads[2].wait()
    send(q.at[:, half(1 - core)], q_mate, core_send.at[1], core_recv.at[1], mate)
    forward_part()
    to_quad()
    for turn in range(ROUNDS):
        hear(turn)
        if turn + 1 < ROUNDS:
            tell(turn + 1)
    to_line()

    arrived(q_mate, core_recv.at[1])
    own.wait()
    for copy in exchange:
        copy.wait_recv()
    state[1, core] = compact(t_dot(q[:, half(core)], g_pair[core]))
    core_in[1] = compact(t_dot(q_mate[...], g_pair[1 - core]))
    to_all()
    send(g_pair.at[1 - core], g.at[core], core_send.at[2], core_recv.at[2], mate)
    g[core] = g_pair[core]
    arrived(g.at[1 - core], core_recv.at[2])
    backward_part()

    to_x(0)
    sent.extend((None, [copy]) for copy in exchange)
    settle()
    to_x(1)
    finish(0)
    for p in range(2):
        prefix = spread(total[0, p].astype(BF16))
        att[:, lanes[p]] = (att_part[:, lanes[p]] + factor * dot(q[:, lanes[p]], prefix)).astype(BF16)
        qg[:, lanes[p]] = (qg_part[:, lanes[p]] + factor * dot_t(g[p], prefix)).astype(BF16)
    settle()
    finish(1)
    suffix[...] = total[1].astype(BF16)


def finish_kernel(factor, att_in, qg_in, kg_part, vg_part, k, v, suffix, att, qg, kg, vg, kg_out, vg_out, sem):
    done = [
        pltpu.make_async_copy(att_in, att, sem.at[0]),
        pltpu.make_async_copy(qg_in, qg, sem.at[1]),
    ]
    for copy in done:
        copy.start()
    for p in range(2):
        lanes = pl.ds(p * PAIR, PAIR)
        later = spread(suffix[p])
        kg_out[:, lanes] = (kg_part[:, lanes] + factor * dot_t(v[:, lanes], later)).astype(BF16)
        vg_out[:, lanes] = (vg_part[:, lanes] + factor * dot(k[:, lanes], later)).astype(BF16)
    for i, (src, dst) in enumerate([(kg_out, kg), (vg_out, vg)]):
        done.append(pltpu.make_async_copy(src, dst, sem.at[2 + i]))
        done[-1].start()
    for copy in done:
        copy.wait()


def on_device(queries, keys, values, out_grad):
    ny = lax.axis_size("head")
    tokens = queries.shape[0] * lax.axis_size("seq")
    factor = 1.0 / math.sqrt(DH * tokens)
    wide = queries.shape
    vmem = pl.BlockSpec(memory_space=pltpu.VMEM)
    hbm = pl.BlockSpec(memory_space=pltpu.HBM)
    pair = (DH, PAIR)
    held = pl.pallas_call(
        functools.partial(carry_kernel, factor, ny),
        out_shape=[
            jax.ShapeDtypeStruct(wide, BF16),
            jax.ShapeDtypeStruct(wide, BF16),
            jax.ShapeDtypeStruct(wide, F32),
            jax.ShapeDtypeStruct(wide, F32),
            jax.ShapeDtypeStruct(wide, BF16),
            jax.ShapeDtypeStruct(wide, BF16),
            jax.ShapeDtypeStruct((2,) + pair, BF16),
        ],
        in_specs=[hbm] * 4,
        out_specs=[vmem] * 7,
        scratch_shapes=[
            pltpu.VMEM(wide, BF16),
            pltpu.VMEM((BLOCK, PAIR), BF16),
            pltpu.VMEM((2, BLOCK, PAIR), BF16),
            pltpu.VMEM((2, BLOCK, PAIR), BF16),
            pltpu.VMEM((4, BLOCK, BLOCK), BF16),
            pltpu.VMEM(wide, F32),
            pltpu.VMEM(wide, F32),
            pltpu.VMEM((2, 2) + pair, F32),
            pltpu.VMEM((2,) + pair, F32),
            pltpu.VMEM((2,) + pair, F32),
            pltpu.VMEM((2,) + pair, BF16),
            pltpu.VMEM((QUAD - 1,) + pair, BF16),
            pltpu.VMEM((4,) + pair, F32),
            pltpu.VMEM(pair, BF16),
            pltpu.VMEM((QUADS - 1,) + pair, BF16),
            pltpu.VMEM((NZ,) + pair, BF16),
            pltpu.VMEM((2,) + pair, BF16),
            pltpu.VMEM((2, 2, NX) + pair, BF16),
            pltpu.VMEM((2,) + pair, F32),
            pltpu.VMEM((2,) + pair, F32),
            pltpu.VMEM((2, 2) + pair, F32),
            pltpu.SemaphoreType.DMA((5,)),
            pltpu.SemaphoreType.DMA((2 * ny,)),
            pltpu.SemaphoreType.DMA((2 * ny,)),
            pltpu.SemaphoreType.DMA((3,)),
            pltpu.SemaphoreType.DMA((3,)),
            pltpu.SemaphoreType.DMA((QUAD - 1,)),
            pltpu.SemaphoreType.DMA((QUAD - 1,)),
            pltpu.SemaphoreType.DMA((QUADS - 1,)),
            pltpu.SemaphoreType.DMA((QUADS - 1,)),
            pltpu.SemaphoreType.DMA((NZ,)),
            pltpu.SemaphoreType.DMA((NZ,)),
            pltpu.SemaphoreType.DMA((2, NX, 2)),
            pltpu.SemaphoreType.DMA((2, 2, NX)),
            pltpu.SemaphoreType.DMA((2,)),
            pltpu.SemaphoreType.DMA((2,)),
            pltpu.SemaphoreType.REGULAR((ROUNDS, 2)),
        ],
        compiler_params=pltpu.CompilerParams(
            collective_id=0, has_side_effects=True, vmem_limit_bytes=16 << 20
        ),
        name="carry",
    )(*[pltpu.with_memory_space_constraint(a, pltpu.HBM) for a in (queries, keys, values, out_grad)])
    return pl.pallas_call(
        functools.partial(finish_kernel, factor),
        out_shape=[jax.ShapeDtypeStruct(wide, BF16)] * 4,
        in_specs=[vmem] * 7,
        out_specs=[hbm] * 4,
        scratch_shapes=[
            pltpu.VMEM(wide, BF16),
            pltpu.VMEM(wide, BF16),
            pltpu.SemaphoreType.DMA((4,)),
        ],
        compiler_params=pltpu.CompilerParams(vmem_limit_bytes=16 << 20),
        name="finish",
    )(*held)


def solution(mesh):
    split = P("seq", "head")
    return jax.shard_map(
        on_device,
        mesh=mesh,
        in_specs=(split, split, split, P(("seq", "head"), None)),
        out_specs=(split, split, split, split),
        check_vma=False,
    )
```

```python
import functools
import math

import jax
import jax.numpy as jnp
from jax import lax
from jax.experimental import pallas as pl
from jax.experimental.pallas import tpu as pltpu
from jax.sharding import PartitionSpec as P

DH = 64
BLOCK = 256
PAIR = 2 * DH
MESH = pl.DeviceIdType.MESH

NX = 4
QUADS = 3
QUAD = 4
NZ = QUADS * QUAD
REACH = 4
ROUNDS = 1

F32 = jnp.float32
BF16 = jnp.bfloat16


def dot(a, b):
    return lax.dot_general(a, b, (((1,), (0,)), ((), ())), preferred_element_type=F32)


def dot_t(a, b):
    return lax.dot_general(a, b, (((1,), (1,)), ((), ())), preferred_element_type=F32)


def t_dot(a, b):
    return lax.dot_general(a, b, (((0,), (0,)), ((), ())), preferred_element_type=F32)


def lane_half(shape):
    return lax.broadcasted_iota(jnp.int32, shape, 1) < DH


def compact(state):
    return jnp.where(lane_half((DH, PAIR)), state[:DH], state[DH:])


def spread(state):
    first = lane_half((DH, PAIR))
    zero = jnp.zeros_like(state)
    return jnp.concatenate([jnp.where(first, state, zero), jnp.where(first, zero, state)], 0)


def halves(a):
    first = lane_half(a.shape)
    zero = jnp.zeros_like(a)
    return jnp.where(first, a, zero), jnp.where(first, zero, a)


def carry_kernel(
    factor, ny,
    q_hbm, k_hbm, v_hbm, g_hbm,
    att, qg, kg_part, vg_part, k, v, suffix,
    q, q_mate, g_pair, g, probs_t, att_part, qg_part,
    state, core_in, chip, chip_out, quad_in, sums, quad_out, line_in, z_in, x_out, x_in, rest_out, rest_in, total,
    load_sem, a2a_send, a2a_recv, core_send, core_recv, quad_send, quad_recv, line_send, line_recv, z_send, z_recv, x_send, x_recv,
    rest_send, rest_recv, heard,
):
    seq, head = lax.axis_index("seq"), lax.axis_index("head")
    core, chip_id = seq % 2, seq // 2
    x, z = chip_id // NZ, chip_id % NZ
    run, place = z // QUAD, z % QUAD
    rows = BLOCK // ny

    def at(x, z, core):
        return (x * NZ + z) * 2 + core

    mate = at(x, z, 1 - core)

    barrier = pltpu.get_barrier_semaphore()
    greeted = [(to, (head + i) % ny) for i in range(1, ny) for to in (seq, mate)] + [(mate, head)]
    near = sorted({i % NZ for i in range(-REACH, REACH + 1)} - {0})
    greeted += [(at(x, (z + i) % NZ, core), head) for i in near]
    greeted += [(at((x + i) % NX, z, c), head) for i in range(1, NX) for c in range(2)]
    for other in greeted:
        pl.semaphore_signal(barrier, inc=1, device_id=other, device_id_type=MESH)

    loads = [
        pltpu.make_async_copy(src, dst, load_sem.at[i])
        for i, (src, dst) in enumerate(
            [(k_hbm, k), (v_hbm, v), (q_hbm, q)]
        )
    ]
    for load in loads:
        load.start()
    pl.semaphore_wait(barrier, len(greeted))

    def tell(turn):
        for i, step in enumerate((REACH, NZ - REACH)):
            to = (at(x, (z + step) % NZ, core), head)
            pl.semaphore_signal(heard.at[turn, i], inc=1, device_id=to, device_id_type=MESH)

    def hear(turn):
        for i in range(2):
            pl.semaphore_wait(heard.at[turn, i], 1)

    mine = pl.ds(pl.multiple_of(head * rows, rows), rows)

    def columns(group, pair):
        return pl.ds(pl.multiple_of((2 * group + pair) * PAIR, PAIR), PAIR)

    exchange = []
    for i in sorted(range(ny), key=lambda i: -min(i, ny - i)):
        there = (head + i) % ny
        for j in range(2):
            if i == 0 and j == 0:
                continue
            exchange.append(
                pltpu.make_async_remote_copy(
                    src_ref=g_hbm.at[:, columns(there, (core + j) % 2)],
                    dst_ref=g_pair.at[core, mine, :],
                    send_sem=a2a_send.at[2 * i + j],
                    recv_sem=a2a_recv.at[2 * i + j],
                    device_id=(at(x, z, (core + j) % 2), there),
                    device_id_type=MESH,
                )
            )
            exchange[-1].start()
    own = pltpu.make_async_copy(
        g_hbm.at[:, columns(head, core)], g_pair.at[core, mine, :], load_sem.at[4]
    )
    own.start()
    tell(0)

    loads[0].wait()
    loads[1].wait()

    lanes = [pl.ds(p * PAIR, PAIR) for p in range(2)]
    for p in range(2):
        state[0, p] = compact(t_dot(k[:, lanes[p]], v[:, lanes[p]]))


    sent = []

    def send(src, dst, send_sem, recv_sem, to, when=None):
        copy = pltpu.make_async_remote_copy(
            src_ref=src,
            dst_ref=dst,
            send_sem=send_sem,
            recv_sem=recv_sem,
            device_id=(to, head),
            device_id_type=MESH,
        )
        if when is None:
            copy.start()
        else:
            pl.when(when)(copy.start)
        sent.append((when, [copy]))

    def settle():
        for when, copies in sent:
            if when is None:
                copies[0].wait_send()
                continue

            @pl.when(when)
            def _():
                for copy in copies:
                    copy.wait_send()

        sent.clear()

    def arrived(ref, sem):
        pltpu.make_async_copy(ref, ref, sem).wait()

    def masked(flag, value):
        return jnp.where(flag, value, jnp.zeros_like(value))

    def before(way, there, here):
        return there < here if way == 0 else there > here

    def half(core):
        return pl.ds(pl.multiple_of(core * PAIR, PAIR), PAIR)

    def chip_sum(way):
        both = state[way, core] + core_in[way]
        chip[way] = both
        chip_out[way] = both.astype(BF16)

    def to_quad():
        arrived(core_in.at[0], core_recv.at[0])
        chip_sum(0)
        for i in range(QUAD - 1):
            send(
                chip_out.at[0], quad_in.at[i], quad_send.at[i], quad_recv.at[i],
                at(x, run * QUAD + (place + 1 + i) % QUAD, core),
            )

    def to_line():
        for i in range(QUAD - 1):
            arrived(quad_in.at[i], quad_recv.at[i])
        whole = chip[0]
        partial = jnp.zeros((DH, PAIR), F32)
        for i in range(QUAD - 1):
            came = quad_in[i].astype(F32)
            whole += came
            partial += masked((place - 1 - i) % QUAD < place, came)
        sums[0] = whole
        sums[1] = partial
        quad_out[...] = whole.astype(BF16)
        for i in range(QUADS - 1):
            send(
                quad_out, line_in.at[i], line_send.at[i], line_recv.at[i],
                at(x, (run + 1 + i) % QUADS * QUAD + place, core),
            )

    def earlier():
        for i in range(QUADS - 1):
            arrived(line_in.at[i], line_recv.at[i])
        whole, partial = sums[0], sums[1]
        for i in range(QUADS - 1):
            came = line_in[i].astype(F32)
            whole += came
            partial += masked((run - 1 - i) % QUADS < run, came)
        return whole, partial

    turn_from = jnp.maximum(z - 2, 0)
    others = [jnp.where(z == 0, 1, 0), jnp.where(z <= 1, 2, 1)]
    others += [2 + (turn_from + i) % (NZ - 2) for i in range(1, NZ - 2)]

    def to_all():
        chip_sum(1)
        for i, there in enumerate(others):
            send(chip_out.at[1], z_in.at[z], z_send.at[i], z_recv.at[z], at(x, there, core),
                jnp.logical_or(there < z, x > 0))

    def later():
        for there in others:
            pl.when(jnp.logical_or(there > z, x > 0))(
                functools.partial(arrived, z_in.at[there], z_recv.at[there])
            )
        whole = chip[1]
        partial = jnp.zeros((DH, PAIR), F32)
        for there in others:
            came = masked(jnp.logical_or(there > z, x > 0), z_in[there].astype(F32))
            whole += came
            partial += masked(there > z, came)
        return whole, partial

    def to_x(way):
        whole, partial = (earlier, later)[way]()
        x_out[way] = whole.astype(BF16)
        for there in range(1, NX) if way == 0 else range(NX - 1):
            copies = [
                pltpu.make_async_remote_copy(
                    src_ref=x_out.at[way],
                    dst_ref=x_in.at[way, core, x],
                    send_sem=x_send.at[way, there, c],
                    recv_sem=x_recv.at[way, core, x],
                    device_id=(at(there, z, c), head),
                    device_id_type=MESH,
                )
                for c in range(2)
            ]

            @pl.when(before(way, x, there))
            def _():
                for copy in copies:
                    copy.start()

            sent.append((before(way, x, there), copies))
        carries = core == 1 - way
        total[way, core] = partial + masked(carries, core_in[way])
        rest_out[way] = partial + masked(jnp.logical_not(carries), state[way, core])
        send(rest_out.at[way], rest_in.at[way], rest_send.at[way], rest_recv.at[way], mate)

    def finish(way):
        arrived(rest_in.at[way], rest_recv.at[way])
        total[way, 1 - core] = rest_in[way]
        for there in range(NX - 1) if way == 0 else range(1, NX):

            @pl.when(before(way, there, x))
            def _():
                for p in range(2):
                    arrived(x_in.at[way, p, there], x_recv.at[way, p, there])
                for p in range(2):
                    total[way, p] += x_in[way, p, there].astype(F32)

    row = lax.broadcasted_iota(jnp.int32, (BLOCK, BLOCK), 0)
    col = lax.broadcasted_iota(jnp.int32, (BLOCK, BLOCK), 1)
    lower, upper = row >= col, row <= col

    def weights(a, b, keep):
        return jnp.where(keep, dot_t(a, b) * factor, 0.0).astype(BF16)

    def forward_part():
        for p in range(2):
            qs, ks, vs = q[:, lanes[p]], k[:, lanes[p]], v[:, lanes[p]]
            kh, vh = halves(ks), halves(vs)
            acc = jnp.zeros((BLOCK, PAIR), F32)
            for h in range(2):
                acc += dot(weights(qs, kh[h], lower), vh[h])
                probs_t[2 * p + h] = weights(kh[h], qs, upper)
            att_part[:, lanes[p]] = acc

    def backward_part():
        for p in range(2):
            qs, ks, vs = (a[:, lanes[p]] for a in (q, k, v))
            gs = g[p]
            qh, kh, vh, gh = halves(qs), halves(ks), halves(vs), halves(gs)
            q_sum = jnp.zeros((BLOCK, PAIR), F32)
            k_sum = jnp.zeros((BLOCK, PAIR), F32)
            v_sum = jnp.zeros((BLOCK, PAIR), F32)
            for h in range(2):
                q_sum += dot(weights(gs, vh[h], lower), kh[h])
                k_sum += dot(weights(vh[h], gs, upper), qh[h])
                v_sum += dot(probs_t[2 * p + h], gh[h])
            qg_part[:, lanes[p]] = q_sum
            kg_part[:, lanes[p]] = k_sum
            vg_part[:, lanes[p]] = v_sum

    send(state.at[0, 1 - core], core_in.at[0], core_send.at[0], core_recv.at[0], mate)
    loads[2].wait()
    send(q.at[:, half(1 - core)], q_mate, core_send.at[1], core_recv.at[1], mate)
    forward_part()
    to_quad()
    for turn in range(ROUNDS):
        hear(turn)
        if turn + 1 < ROUNDS:
            tell(turn + 1)
    to_line()

    arrived(q_mate, core_recv.at[1])
    own.wait()
    for copy in exchange:
        copy.wait_recv()
    state[1, core] = compact(t_dot(q[:, half(core)], g_pair[core]))
    core_in[1] = compact(t_dot(q_mate[...], g_pair[1 - core]))
    to_all()
    send(g_pair.at[1 - core], g.at[core], core_send.at[2], core_recv.at[2], mate)
    g[core] = g_pair[core]
    arrived(g.at[1 - core], core_recv.at[2])
    backward_part()

    to_x(0)
    sent.extend((None, [copy]) for copy in exchange)
    settle()
    to_x(1)
    finish(0)
    for p in range(2):
        prefix = spread(total[0, p].astype(BF16))
        att[:, lanes[p]] = (att_part[:, lanes[p]] + factor * dot(q[:, lanes[p]], prefix)).astype(BF16)
        qg[:, lanes[p]] = (qg_part[:, lanes[p]] + factor * dot_t(g[p], prefix)).astype(BF16)
    settle()
    finish(1)
    suffix[...] = total[1].astype(BF16)


def finish_kernel(factor, att_in, qg_in, kg_part, vg_part, k, v, suffix, att, qg, kg, vg, kg_out, vg_out, sem):
    done = [
        pltpu.make_async_copy(att_in, att, sem.at[0]),
        pltpu.make_async_copy(qg_in, qg, sem.at[1]),
    ]
    for copy in done:
        copy.start()
    for p in range(2):
        lanes = pl.ds(p * PAIR, PAIR)
        later = spread(suffix[p])
        kg_out[:, lanes] = (kg_part[:, lanes] + factor * dot_t(v[:, lanes], later)).astype(BF16)
        vg_out[:, lanes] = (vg_part[:, lanes] + factor * dot(k[:, lanes], later)).astype(BF16)
    for i, (src, dst) in enumerate([(kg_out, kg), (vg_out, vg)]):
        done.append(pltpu.make_async_copy(src, dst, sem.at[2 + i]))
        done[-1].start()
    for copy in done:
        copy.wait()


def on_device(queries, keys, values, out_grad):
    ny = lax.axis_size("head")
    tokens = queries.shape[0] * lax.axis_size("seq")
    factor = 1.0 / math.sqrt(DH * tokens)
    wide = queries.shape
    vmem = pl.BlockSpec(memory_space=pltpu.VMEM)
    hbm = pl.BlockSpec(memory_space=pltpu.HBM)
    pair = (DH, PAIR)
    held = pl.pallas_call(
        functools.partial(carry_kernel, factor, ny),
        out_shape=[
            jax.ShapeDtypeStruct(wide, BF16),
            jax.ShapeDtypeStruct(wide, BF16),
            jax.ShapeDtypeStruct(wide, F32),
            jax.ShapeDtypeStruct(wide, F32),
            jax.ShapeDtypeStruct(wide, BF16),
            jax.ShapeDtypeStruct(wide, BF16),
            jax.ShapeDtypeStruct((2,) + pair, BF16),
        ],
        in_specs=[hbm] * 4,
        out_specs=[vmem] * 7,
        scratch_shapes=[
            pltpu.VMEM(wide, BF16),
            pltpu.VMEM((BLOCK, PAIR), BF16),
            pltpu.VMEM((2, BLOCK, PAIR), BF16),
            pltpu.VMEM((2, BLOCK, PAIR), BF16),
            pltpu.VMEM((4, BLOCK, BLOCK), BF16),
            pltpu.VMEM(wide, F32),
            pltpu.VMEM(wide, F32),
            pltpu.VMEM((2, 2) + pair, F32),
            pltpu.VMEM((2,) + pair, F32),
            pltpu.VMEM((2,) + pair, F32),
            pltpu.VMEM((2,) + pair, BF16),
            pltpu.VMEM((QUAD - 1,) + pair, BF16),
            pltpu.VMEM((4,) + pair, F32),
            pltpu.VMEM(pair, BF16),
            pltpu.VMEM((QUADS - 1,) + pair, BF16),
            pltpu.VMEM((NZ,) + pair, BF16),
            pltpu.VMEM((2,) + pair, BF16),
            pltpu.VMEM((2, 2, NX) + pair, BF16),
            pltpu.VMEM((2,) + pair, F32),
            pltpu.VMEM((2,) + pair, F32),
            pltpu.VMEM((2, 2) + pair, F32),
            pltpu.SemaphoreType.DMA((5,)),
            pltpu.SemaphoreType.DMA((2 * ny,)),
            pltpu.SemaphoreType.DMA((2 * ny,)),
            pltpu.SemaphoreType.DMA((3,)),
            pltpu.SemaphoreType.DMA((3,)),
            pltpu.SemaphoreType.DMA((QUAD - 1,)),
            pltpu.SemaphoreType.DMA((QUAD - 1,)),
            pltpu.SemaphoreType.DMA((QUADS - 1,)),
            pltpu.SemaphoreType.DMA((QUADS - 1,)),
            pltpu.SemaphoreType.DMA((NZ,)),
            pltpu.SemaphoreType.DMA((NZ,)),
            pltpu.SemaphoreType.DMA((2, NX, 2)),
            pltpu.SemaphoreType.DMA((2, 2, NX)),
            pltpu.SemaphoreType.DMA((2,)),
            pltpu.SemaphoreType.DMA((2,)),
            pltpu.SemaphoreType.REGULAR((ROUNDS, 2)),
        ],
        compiler_params=pltpu.CompilerParams(
            collective_id=0, has_side_effects=True, vmem_limit_bytes=16 << 20
        ),
        name="carry",
    )(*[pltpu.with_memory_space_constraint(a, pltpu.HBM) for a in (queries, keys, values, out_grad)])
    return pl.pallas_call(
        functools.partial(finish_kernel, factor),
        out_shape=[jax.ShapeDtypeStruct(wide, BF16)] * 4,
        in_specs=[vmem] * 7,
        out_specs=[hbm] * 4,
        scratch_shapes=[
            pltpu.VMEM(wide, BF16),
            pltpu.VMEM(wide, BF16),
            pltpu.SemaphoreType.DMA((4,)),
        ],
        compiler_params=pltpu.CompilerParams(vmem_limit_bytes=16 << 20),
        name="finish",
    )(*held)


def solution(mesh):
    split = P("seq", "head")
    return jax.shard_map(
        on_device,
        mesh=mesh,
        in_specs=(split, split, split, P(("seq", "head"), None)),
        out_specs=(split, split, split, split),
        check_vma=False,
    )
```
